32 devices in a mesh: band: 4 (over y, x), dom: 8 (over z, core).
Axes of the slice: x: 2, y: 2, z: 4, core: 2. Of those that a mesh axis runs over, the one named last changes fastest.
Arguments:
- orbitals: float32 [1024, 32768], P('band', 'dom'), may hold values from -6 to 6
- projectors: float32 [256, 512, 128], P('dom'), may hold values from -0.25 to 0.25
- window_start: int32 [256], P('dom'), may hold values from 0 to 3584
- slot_atom: int32 [8, 32], replicated, may hold values from 0 to 23, as said below
- atom_home: int32 [24], replicated, may hold values from 0 to 23, as said below
- atom_matrices: float32 [24, 128, 128], P('dom'), may hold values from -0.1875 to 0.1875
- rotation: float32 [1024, 1024], P('band'), may hold values from -0.1875 to 0.1875
Outputs:
- rotated: float32 [1024, 32768], P('band', 'dom')
The draws below stay inside these ranges and needn't reach their ends.
Inputs may be any that keep to these rules, and one draw needn't show every extreme that they name: `atom_home`: a permutation; atom a is owned by domain atom_home[a] // 3, so every domain owns 3 atoms. `slot_atom`: in one domain at most 8 windows have atoms of one owner; in every domain some owner has exactly 8 of them, and some owner has exactly 8 from every domain.
All inputs are finite; a program needn't handle non-finite values.
Results may differ from the reference program's by a relative error of at most 0.0003.
Values sent between devices are 32-bit elements; how exact they have to be, the bound alone decides.
No kernel may reach another device: no remote copies, remote signals or barrier semaphores. Data moves between devices by JAX's collectives and lax.ppermute only.
A program may use at most 128 MiB of HBM per device.

```python
import jax
import jax.numpy as jnp
from jax import lax

BANDS = 1024
PROJS = 128
WINDOW = 512
CELLS = 4096
SLOTS = 32
ATOM_DEV = 3
GRID = 32768
ATOMS = 24
CAPACITY = 8
N_DOM = 8


def intersection_layout(key):
    folded = jax.random.fold_in(key, 4242)
    key_home, key_full, key_second, key_rank, key_order, key_pick = jax.random.split(folded, 6)
    domains = ATOMS // ATOM_DEV
    places = domains * CAPACITY
    atom_home = jax.random.permutation(key_home, ATOMS).astype(jnp.int32)
    atom_at_row = jnp.argsort(atom_home).astype(jnp.int32)
    shared = jax.random.randint(key_full, (), 0, domains)
    second_owner = jax.random.randint(key_second, (domains, 1), 0, domains)
    ranking = jax.vmap(lambda subkey: jax.random.permutation(subkey, places))(jax.random.split(key_rank, domains)).astype(jnp.int32)
    positions = jnp.arange(places, dtype=jnp.int32)[None, :]
    owner_of = positions // CAPACITY
    within = positions % CAPACITY
    priority = ranking + 2 * places
    priority = jnp.where(owner_of == second_owner, CAPACITY + within, priority)
    priority = jnp.where(owner_of == shared, within, priority)
    chosen = jnp.argsort(priority, axis=1)[:, :SLOTS].astype(jnp.int32)
    mixing = jax.vmap(lambda subkey: jax.random.permutation(subkey, SLOTS))(jax.random.split(key_order, domains))
    chosen = jnp.take_along_axis(chosen, mixing, axis=1)
    owners = chosen // CAPACITY
    atom_pick = jax.random.randint(key_pick, (domains, SLOTS), 0, ATOM_DEV)
    slot_atom = atom_at_row[owners * ATOM_DEV + atom_pick]
    return (atom_home, slot_atom.astype(jnp.int32))


def draw_slot_atom(key, part):
    return intersection_layout(key)[1]


def draw_atom_home(key, part):
    return intersection_layout(key)[0]


def with_ends(array, stream_key, low, largest):
    place = [jax.random.randint(jax.random.fold_in(stream_key, axis), (), 0, length) for axis, length in enumerate(array.shape)]
    widest = array.shape.index(max(array.shape))
    next_to = place[:widest] + [(place[widest] + 1) % array.shape[widest]] + place[widest + 1:]
    return array.at[tuple(place)].set(low).at[tuple(next_to)].set(largest)


def shard_levels(rng, extent, cuts, least, largest):
    gain = 1.0
    for position, parts in cuts:
        steps = jax.random.uniform(jax.random.fold_in(jax.random.fold_in(rng, 6), position), (parts,), jnp.float32, least / len(cuts), largest / len(cuts))
        gain = gain * jnp.repeat(jnp.exp(steps), extent[position] // parts).reshape((-1,) + (1,) * (len(extent) - 1 - position))
    return gain


def scatter_about(stream_key, shape, spread, limit, shards=(), kind=jnp.bfloat16):
    level = shard_levels(stream_key, shape, shards, -0.22, 0.18) if shards else 1.0
    entries = jax.random.normal(stream_key, shape, jnp.float32) * spread * level
    return jnp.minimum(jnp.maximum(entries, -limit), limit).astype(kind)


def setup_inputs(seed: int = 0) -> dict:
    streams_of = jax.random.split(jax.random.key(seed), 8)
    orbitals = scatter_about(streams_of[0], (BANDS, GRID), 1.0, 6.0, ((0, 4), (1, 8)), jnp.float32)
    projectors = scatter_about(streams_of[1], (N_DOM * SLOTS, WINDOW, PROJS), WINDOW ** -0.5, 0.25, ((0, 8),), jnp.float32)
    window_start = with_ends(jax.random.randint(streams_of[2], (N_DOM * SLOTS,), 0, CELLS - WINDOW + 1), jax.random.fold_in(streams_of[2], 1), 0, CELLS - WINDOW).astype(jnp.int32)
    slot_atom = draw_slot_atom(jax.random.fold_in(streams_of[7], 71), 0)
    atom_home = draw_atom_home(jax.random.fold_in(streams_of[7], 71), 0)
    atom_matrices = scatter_about(streams_of[5], (ATOMS, PROJS, PROJS), (8 * PROJS) ** -0.5, 0.1875, ((0, 8),), jnp.float32)
    rotation = scatter_about(streams_of[6], (BANDS, BANDS), BANDS ** -0.5, 0.1875, ((0, 4),), jnp.float32)
    return dict(orbitals=orbitals, projectors=projectors, window_start=window_start, slot_atom=slot_atom, atom_home=atom_home, atom_matrices=atom_matrices, rotation=rotation)


HIGHEST = lax.Precision.HIGHEST


def reference(orbitals, projectors, window_start, slot_atom, atom_home, atom_matrices, rotation):
    atom_ids = jnp.arange(ATOMS, dtype=jnp.int32)

    def domain_pieces(domain):
        domain = domain.astype(jnp.int32)
        block = lax.dynamic_slice_in_dim(orbitals, domain * CELLS, CELLS, 1)
        starts = lax.dynamic_slice_in_dim(window_start, domain * SLOTS, SLOTS, 0)
        tiles = lax.dynamic_slice_in_dim(projectors, domain * SLOTS, SLOTS, 0)
        members = lax.dynamic_index_in_dim(slot_atom, domain, 0, keepdims=False)
        return block, starts, tiles, members

    def accumulate(domain, totals):
        block, starts, tiles, members = domain_pieces(domain)
        windows = jax.vmap(lambda offset: lax.dynamic_slice_in_dim(block, offset, WINDOW, 1))(starts)
        partials = jnp.einsum("sbw,swp->sbp", windows, tiles, precision=HIGHEST)
        matching = (atom_ids[:, None] == members[None, :]).astype(jnp.float32)
        return totals + jnp.einsum("as,sbp->abp", matching, partials, precision=HIGHEST)

    atom_sums = lax.fori_loop(0, N_DOM, accumulate, jnp.zeros((ATOMS, BANDS, PROJS), jnp.float32))
    matrices = atom_matrices[atom_home]
    factors = jnp.einsum("abp,apq->abq", atom_sums, matrices, precision=HIGHEST)

    def correct(domain):
        block, starts, tiles, members = domain_pieces(domain)
        slot_factors = factors[members]
        updates = jnp.einsum("sbq,swq->sbw", slot_factors, tiles, precision=HIGHEST)

        def add_window(slot_index, current):
            offset = starts[slot_index]
            previous = lax.dynamic_slice_in_dim(current, offset, WINDOW, 1)
            return lax.dynamic_update_slice_in_dim(current, previous + updates[slot_index], offset, 1)

        return lax.fori_loop(0, SLOTS, add_window, block)

    corrected_blocks = lax.map(correct, jnp.arange(N_DOM, dtype=jnp.int32))
    corrected = jnp.transpose(corrected_blocks, (1, 0, 2)).reshape(BANDS, GRID)
    return jnp.dot(rotation, corrected, precision=HIGHEST, preferred_element_type=jnp.float32)
```

```python
import functools

import jax
import jax.numpy as jnp
from jax import lax
from jax.experimental import pallas as pl
from jax.experimental.pallas import tpu as pltpu
from jax.sharding import PartitionSpec as P


F32 = jnp.float32
BF16 = jnp.bfloat16
LANES = 128
ANY = pl.BlockSpec(memory_space=pl.ANY)
VMEM_LIMIT = 60 * 1024 * 1024


def split(value):
    high = value.astype(BF16)
    return high, (value - high.astype(F32)).astype(BF16)


def dot(a, b, contract=((1,), (0,))):
    return lax.dot_general(a, b, (contract, ((), ())), preferred_element_type=F32)


def dot3(a, b):
    (ah, al), (bh, bl) = a, b
    return dot(ah, bh) + dot(ah, bl) + dot(al, bh)


def params(**kwargs):
    return pltpu.CompilerParams(vmem_limit_bytes=VMEM_LIMIT, **kwargs)


def cost(flops, size):
    return pl.CostEstimate(flops=int(flops), bytes_accessed=int(size), transcendentals=0)


def shifted(tile, shift):
    wide = jnp.concatenate([tile, jnp.zeros((LANES, tile.shape[1]), F32)], axis=0)
    return pltpu.roll(wide, shift, 0)


def project_kernel(group, parts, meta, x_ref, proj_ref, *refs):
    outs, (high, low, sums, sem) = refs[: len(parts)], refs[len(parts) :]
    step = pl.program_id(0)
    span = proj_ref.shape[1] + LANES

    @pl.when(step == 0)
    def _():
        sums[...] = jnp.zeros_like(sums)
        width = 512

        def cut(i, _):
            at = pl.ds(pl.multiple_of(i * width, width), width)
            high[:, at], low[:, at] = split(x_ref[:, at])
            return 0

        lax.fori_loop(0, x_ref.shape[1] // width, cut, 0)

    for i in range(group):
        slot = step * group + i
        at = pl.ds(pl.multiple_of(meta[0, slot] * LANES, LANES), span)
        ph, pll = split(shifted(proj_ref[i], meta[1, slot]))
        both = dot(high[:, at], jnp.concatenate([ph, pll], axis=1))
        half = both.shape[1] // 2
        sums[meta[2, slot]] += both[:, :half] + both[:, half:] + dot(low[:, at], ph)

    @pl.when(step == pl.num_programs(0) - 1)
    def _():
        copies = [
            pltpu.make_async_copy(sums.at[pl.ds(start, size)], out, sem.at[n])
            for n, (out, (start, size)) in enumerate(zip(outs, parts))
        ]
        for copy in copies:
            copy.start()
        for copy in copies:
            copy.wait()


def project(meta, orbitals, projectors, rows, parts, group=4):
    bands, cells = orbitals.shape
    slots, window, projs = projectors.shape
    spec = pltpu.PrefetchScalarGridSpec(
        num_scalar_prefetch=1,
        grid=(slots // group,),
        in_specs=[
            pl.BlockSpec((bands, cells), lambda i, m: (0, 0)),
            pl.BlockSpec((group, window, projs), lambda i, m: (i, 0, 0)),
        ],
        out_specs=[ANY] * len(parts),
        scratch_shapes=[
            pltpu.VMEM((bands, cells), BF16),
            pltpu.VMEM((bands, cells), BF16),
            pltpu.VMEM((rows, bands, projs), F32),
            pltpu.SemaphoreType.DMA((len(parts),)),
        ],
    )
    return pl.pallas_call(
        functools.partial(project_kernel, group, parts),
        grid_spec=spec,
        out_shape=[jax.ShapeDtypeStruct((n, bands, projs), F32) for _, n in parts],
        compiler_params=params(),
        cost_estimate=cost(
            8 * slots * bands * window * projs, 4 * (orbitals.size + projectors.size)
        ),
        name="project",
    )(meta, orbitals, projectors)


def rotate_kernel(rot_ref, x_ref, y_ref, out_ref):
    cols = jnp.concatenate([x_ref[...], y_ref[...]], axis=0)
    out_ref[...] = dot3(split(rot_ref[...]), split(cols))


def rotate(rot, x, y, start, width, block):
    bands = x.shape[0]
    first = start // block
    spec = pl.BlockSpec((bands, block), lambda i: (0, first + i))
    return pl.pallas_call(
        rotate_kernel,
        grid=(width // block,),
        in_specs=[pl.BlockSpec(rot.shape, lambda i: (0, 0)), spec, spec],
        out_specs=pl.BlockSpec((rot.shape[0], block), lambda i: (0, i)),
        out_shape=jax.ShapeDtypeStruct((rot.shape[0], width), F32),
        compiler_params=params(),
        cost_estimate=cost(6 * rot.size * width, 4 * (3 * bands * width + rot.size)),
        name="rotate",
    )(rot, x, y)


def factor_kernel(a_ref, b_ref, matrix_ref, out_ref):
    for i in range(a_ref.shape[0]):
        out_ref[i] = dot3(split(a_ref[i] + b_ref[i]), split(matrix_ref[i]))


def factor(a, b, matrices):
    return pl.pallas_call(
        factor_kernel,
        out_shape=jax.ShapeDtypeStruct(a.shape, F32),
        compiler_params=params(),
        cost_estimate=cost(6 * a.size * a.shape[2], 12 * a.size),
        name="factor",
    )(a, b, matrices)


def turn_kernel(other_ref, mine_ref, a_ref, b_ref, sent_ref, kept_ref):
    other, mine = split(other_ref[...]), split(mine_ref[...])
    for i in range(a_ref.shape[0]):
        cols = split(jnp.concatenate([a_ref[i], b_ref[i]], axis=0))
        sent_ref[i] = dot3(other, cols)
        kept_ref[i] = dot3(mine, cols)


def turn(other, mine, a, b):
    shape = jax.ShapeDtypeStruct(a.shape, F32)
    return pl.pallas_call(
        turn_kernel,
        out_shape=[shape, shape],
        compiler_params=params(),
        cost_estimate=cost(12 * other.size * a.shape[0] * a.shape[2], 16 * a.size),
        name="turn",
    )(other, mine, a, b)


def correct_kernel(group, parts, meta, base_ref, proj_ref, *refs):
    ins, (out_ref, factors, sem) = refs[: len(parts)], refs[len(parts) :]
    step = pl.program_id(0)
    span = proj_ref.shape[1] + LANES

    @pl.when(step == 0)
    def _():
        copies = [pltpu.make_async_copy(base_ref, out_ref, sem.at[len(parts)])]
        copies += [
            pltpu.make_async_copy(part, factors.at[pl.ds(start, size)], sem.at[n])
            for n, (part, (start, size)) in enumerate(zip(ins, parts))
        ]
        for copy in copies:
            copy.start()
        for copy in copies:
            copy.wait()

    for i in range(group):
        slot = step * group + i
        at = pl.ds(pl.multiple_of(meta[0, slot] * LANES, LANES), span)
        ph, pll = split(shifted(proj_ref[i], meta[1, slot]))
        fh, fl = split(factors[meta[2, slot]])
        rows = ((1,), (1,))
        both = dot(jnp.concatenate([fh, fl], axis=1), jnp.concatenate([ph, ph], axis=1), rows)
        out_ref[:, at] += both + dot(fh, pll, rows)


def correct(meta, base, projectors, factors, rows, parts, group=4):
    bands, cells = base.shape
    slots, window, projs = projectors.shape
    spec = pltpu.PrefetchScalarGridSpec(
        num_scalar_prefetch=1,
        grid=(slots // group,),
        in_specs=[ANY, pl.BlockSpec((group, window, projs), lambda i, m: (i, 0, 0))]
        + [ANY] * len(parts),
        out_specs=pl.BlockSpec((bands, cells), lambda i, m: (0, 0)),
        scratch_shapes=[
            pltpu.VMEM((rows, bands, projs), F32),
            pltpu.SemaphoreType.DMA((len(parts) + 1,)),
        ],
    )
    return pl.pallas_call(
        functools.partial(correct_kernel, group, parts),
        grid_spec=spec,
        out_shape=jax.ShapeDtypeStruct((bands, cells), F32),
        compiler_params=params(),
        cost_estimate=cost(
            8 * slots * bands * window * projs, 4 * (2 * base.size + projectors.size)
        ),
        name="correct",
    )(meta, base, projectors, *factors)


def add_kernel(whole_ref, part_ref, out_ref):
    out_ref[...] = whole_ref[...] + part_ref[...]


def add_columns(whole, part, start, block):
    bands, width = part.shape
    first = start // block
    wide = pl.BlockSpec((bands, block), lambda i: (0, first + i))
    return pl.pallas_call(
        add_kernel,
        grid=(width // block,),
        in_specs=[wide, pl.BlockSpec((bands, block), lambda i: (0, i))],
        out_specs=wide,
        out_shape=jax.ShapeDtypeStruct(whole.shape, F32),
        input_output_aliases={0: 0},
        compiler_params=params(),
        cost_estimate=cost(part.size, 12 * part.size),
        name="add_columns",
    )(whole, part)


def per_device(
    sizes, orbitals, projectors, window_start, slot_atom, atom_home, atom_matrices, rotation
):
    groups, domains = sizes
    bands, cells = orbitals.shape
    slots, window, projs = projectors.shape
    owned = atom_matrices.shape[0]
    bits = domains.bit_length() - 1
    group = lax.axis_index("band")
    domain = lax.axis_index("dom")
    first_bit = 1 + (domain & 1)
    second_bit = 3 - first_bit

    def send(value, partner):
        pairs = [
            (g * domains + d, partner(g, d)[0] * domains + partner(g, d)[1])
            for g in range(groups)
            for d in range(domains)
        ]
        return lax.ppermute(value, ("band", "dom"), pairs)

    def to_first(value):
        return send(value, lambda g, d: (g ^ (1 + (d & 1)), d))

    def to_second(value):
        return send(value, lambda g, d: (g ^ (2 - (d & 1)), d))

    def to_domain(value, bit):
        return send(value, lambda g, d: (g, d ^ (1 << bit)))

    def columns_of(which):
        return lax.dynamic_slice_in_dim(rotation, which * bands, bands, 1)

    others = to_first(orbitals)
    mine = jnp.concatenate([columns_of(group), columns_of(group ^ first_bit)], axis=1)
    theirs = jnp.concatenate([columns_of(group ^ second_bit), columns_of(group ^ 3)], axis=1)
    theirs = to_second(theirs)

    pieces = [(0, 1), (1, owned)] if owned > 1 else [(0, 1)]
    start_block = jnp.minimum(window_start // LANES, (cells - window - LANES) // LANES)
    atoms = lax.dynamic_index_in_dim(slot_atom, domain, 0, keepdims=False)
    ids = jnp.arange(atom_home.shape[0], dtype=jnp.int32)
    home = jnp.sum(jnp.where(atoms[:, None] == ids[None, :], atom_home[None, :], 0), axis=1)
    owner, which = home // owned, home % owned
    apart = owner ^ domain
    order = sum(((apart >> t) & 1) << (bits - 1 - t) for t in range(bits))
    row = jnp.zeros_like(order)
    parts = []
    for low, high in pieces:
        size = (high - low) * domains
        row = jnp.where(
            (which >= low) & (which < high),
            low * domains + order * (high - low) + which - low,
            row,
        )
        parts += [(low * domains, size // 2), (low * domains + size // 2, size // 2)]
    meta = jnp.stack([start_block, window_start - start_block * LANES, row]).astype(jnp.int32)
    rows = owned * domains

    sums = project(meta, orbitals, projectors, rows, parts)

    gathered = []
    for n, (low, high) in enumerate(pieces):
        kept, sent = sums[2 * n], sums[2 * n + 1]
        for bit in range(bits):
            got = to_domain(sent, bit)
            if bit == bits - 1:
                break
            half = kept.shape[0] // 2
            sent = kept[half:] + got[half:]
            kept = kept[:half] + got[:half]
        mixed = factor(kept, got, atom_matrices[low:high])
        turned_sent, turned = turn(theirs, mine, mixed, to_first(mixed))
        whole = turned + to_second(turned_sent)
        for bit in reversed(range(bits)):
            other = to_domain(whole, bit)
            if bit == 0:
                gathered += [whole, other]
            else:
                whole = jnp.concatenate([whole, other], axis=0)

    block = 512
    chunks = []
    at = 0
    for width in chunk_widths(cells, block):
        chunks.append((at, width))
        at += width
    received = []
    for at, width in chunks:
        received.append(to_second(rotate(theirs, orbitals, others, at, width, block)))
    base = rotate(mine, orbitals, others, 0, cells, block)
    result = correct(meta, base, projectors, gathered, rows, parts)
    for (at, width), part in zip(chunks, received):
        result = add_columns(result, part, at, block)
    return result


def chunk_widths(cells, block):
    left = cells // block
    widths = [1]
    while sum(widths) < left - 1:
        widths.append(min(2, left - 1 - sum(widths)))
    return [w * block for w in widths + [1]]


def solution(mesh):
    in_specs = (
        P("band", "dom"),
        P("dom", None, None),
        P("dom"),
        P(),
        P(),
        P("dom", None, None),
        P("band", None),
    )
    sizes = (mesh.shape["band"], mesh.shape["dom"])
    return jax.shard_map(
        functools.partial(per_device, sizes),
        mesh=mesh,
        in_specs=in_specs,
        out_specs=P("band", "dom"),
        check_vma=False,
    )
```
